512 devices in a mesh: col: 128 (over y, z, core), lev: 4 (over x).
Axes of the slice: x: 4, y: 8, z: 8, core: 2. Of those that a mesh axis runs over, the one named last changes fastest.
Arguments:
- fields: bfloat16 [2, 32, 131072], P(None, 'lev', 'col'), may hold values from 0.5 to 3
- bracket: int32 [8, 131072], P(None, 'col'), may hold values from 0 to 30
- fraction: float32 [8, 131072], P(None, 'col'), may hold values from 0 to 1
- remap_weights: bfloat16 [2048, 128, 128], P('col'), may hold values from 0 to 0.015625
- intersections: int32 [3, 4096], P(None, 'col'), may hold values from 0 to 1023, as said below
- tile_owner: int32 [1024], replicated, may hold values from 0 to 1023, as said below
Outputs:
- normalized: float32 [2, 8, 1024, 128], P(None, 'lev', 'col')
The draws below stay inside these ranges and needn't reach their ends.
Inputs may be any that keep to these rules, and one draw needn't show every extreme that they name: `intersections`: row 0 names a source block of the entry's own col index; row 1 a target tile whose owner, tile_owner[tile] // 8, lies within 2 indices of the entry's col index or exactly 64 indices away, cyclically; row 2 a weight block of the entry's own col index. `tile_owner`: A permutation of the tiles.
All inputs are finite; a program needn't handle non-finite values.
Results may differ from the reference program's by a relative error of at most 0.00031.
Values may be sent and summed in bfloat16 or wider, within the bound.
No kernel may reach another device: no remote copies, remote signals or barrier semaphores. Data moves between devices by JAX's collectives and lax.ppermute only.
A program may use at most 64 MiB of HBM per device.

```python
import jax
import jax.numpy as jnp
from jax import lax

F = 2
LEV = 32
PLEV = 8
BLK = 128
TILE = 128
HALF = 2
BLK_DEV = 8
TILE_DEV = 8
ENT_DEV = 32
WB_DEV = 16
COLS = 131072
TILES = 1024
ENT = 4096
WB = 2048
N_COL = 128


def intersection_layout(key):
    order = jax.random.permutation(jax.random.fold_in(key, 11), TILES).astype(jnp.int32)
    tile_at = jnp.argsort(order).astype(jnp.int32)
    entry_total = ENT_DEV * N_COL
    entry_ids = jnp.arange(entry_total, dtype=jnp.int32)
    device = entry_ids // ENT_DEV
    near = jax.random.randint(jax.random.fold_in(key, 12), (entry_total,), -HALF, HALF + 1).astype(jnp.int32)
    offset = jnp.where(entry_ids % ENT_DEV == 0, N_COL // 2, near).astype(jnp.int32)
    local_tile = jax.random.randint(jax.random.fold_in(key, 13), (entry_total,), 0, TILE_DEV).astype(jnp.int32)
    owner_dev = (device + offset + N_COL) % N_COL
    target = jnp.take(tile_at, owner_dev * TILE_DEV + local_tile)
    source = jax.random.randint(jax.random.fold_in(key, 14), (entry_total,), 0, BLK_DEV).astype(jnp.int32)
    block_id = jax.random.randint(jax.random.fold_in(key, 15), (entry_total,), 0, WB_DEV).astype(jnp.int32)
    return (order, jnp.stack([source, target, block_id]).astype(jnp.int32))


def draw_intersections(key, part):
    return intersection_layout(key)[1]


def draw_tile_owner(key, part):
    return intersection_layout(key)[0]


def plant(result, own_key, smallest, high):
    dims = result.shape
    spot = [jax.random.randint(jax.random.fold_in(own_key, axis), (), 0, dims[axis]) for axis in range(len(dims))]
    result = result.at[tuple(spot)].set(smallest)
    longest = dims.index(max(dims))
    spot[longest] = (spot[longest] + 1) % dims[longest]
    return result.at[tuple(spot)].set(high)


def steps_of(key, extent, shards, least, top_value):
    def one(axis_at, shards_of):
        steps = jax.random.uniform(jax.random.fold_in(jax.random.fold_in(key, 6), axis_at), (shards_of,), jnp.float32, least / len(shards), top_value / len(shards))
        return jnp.repeat(jnp.exp(steps), extent[axis_at] // shards_of).reshape((-1,) + (1,) * (len(extent) - axis_at - 1))

    level = one(*shards[0])
    for cut in shards[1:]:
        level = level * one(*cut)
    return level


def setup_inputs(seed: int = 0) -> dict:
    seeds = jax.random.split(jax.random.key(seed), 7)
    return {
        "fields": jnp.clip(0.5 + 2.5 * jax.random.uniform(seeds[0], (F, LEV, COLS), jnp.float32) ** steps_of(seeds[0], (F, LEV, COLS), ((1, 4), (2, 128)), -0.2, 0.2), 0.5, 3.0).astype(jnp.bfloat16),
        "bracket": plant(jax.random.randint(seeds[1], (PLEV, COLS), 0, LEV - 1), jax.random.fold_in(seeds[1], 1), 0, (LEV - 1) - 1).astype(jnp.int32),
        "fraction": jnp.clip(1.0 * jax.random.uniform(seeds[2], (PLEV, COLS), jnp.float32) ** steps_of(seeds[2], (PLEV, COLS), ((1, 128),), -0.2, 0.2), 0.0, 1.0),
        "remap_weights": jnp.clip(0.015625 * jax.random.uniform(seeds[3], (WB, BLK, TILE), jnp.float32) ** steps_of(seeds[3], (WB, BLK, TILE), ((0, 128),), -0.2, 0.2), 0.0, 0.015625).astype(jnp.bfloat16),
        "intersections": draw_intersections(jax.random.fold_in(seeds[6], 71), 0),
        "tile_owner": draw_tile_owner(jax.random.fold_in(seeds[6], 71), 0),
    }


epsilon = 1e-06

def reference(fields, bracket, fraction, remap_weights, intersections, tile_owner):
    values = fields.astype(jnp.float32)
    lower_index = jnp.broadcast_to(bracket[None], (F, PLEV, COLS))
    below_vals = jnp.take_along_axis(values, lower_index, axis=1)
    above_vals = jnp.take_along_axis(values, lower_index + 1, axis=1)
    interp = ((1.0 - fraction[None]) * below_vals + fraction[None] * above_vals).astype(jnp.bfloat16)
    blocks = interp.reshape(F, PLEV, N_COL, BLK_DEV, BLK).transpose(2, 0, 1, 3, 4)
    entry_lists = intersections.reshape(3, N_COL, ENT_DEV).transpose(1, 0, 2)
    weight_sets = remap_weights.reshape(N_COL, WB_DEV, BLK, TILE)

    def per_device(packed):
        block_set, entry_set, weight_set = packed
        chosen = jnp.take(block_set, entry_set[0], axis=2).astype(jnp.float32)
        picked = jnp.take(weight_set, entry_set[2], axis=0).astype(jnp.float32)
        return jnp.einsum('fpeb,ebt->efpt', chosen, picked, precision=lax.Precision.HIGHEST)
    parts = lax.map(per_device, (blocks, entry_lists, weight_sets))
    parts = parts.reshape(ENT, F, PLEV, TILE)
    slot_index = jnp.take(tile_owner, intersections[1])
    remapped = jax.ops.segment_sum(parts, slot_index, num_segments=TILES)
    remapped = remapped.transpose(1, 2, 0, 3)
    shifted_left = jnp.concatenate([remapped[..., :1], remapped[..., :-1]], axis=-1)
    shifted_right = jnp.concatenate([remapped[..., 1:], remapped[..., -1:]], axis=-1)
    filtered = 0.25 * shifted_left + 0.5 * remapped + 0.25 * shifted_right
    cells = float(TILES * TILE)
    field_mean = lax.optimization_barrier(jnp.sum(filtered, axis=(2, 3))) / cells
    centered = filtered - field_mean[:, :, None, None]
    field_var = lax.optimization_barrier(jnp.sum(centered * centered, axis=(2, 3))) / cells
    return centered * lax.rsqrt(field_var + epsilon)[:, :, None, None]
```

```python
import jax
import jax.numpy as jnp
from jax import lax
from jax.experimental import pallas as pl
from jax.experimental.pallas import tpu as pltpu
from jax.sharding import PartitionSpec as P

F = 2
PLEV = 8
GROUP = 4
CROSS = 2

epsilon = 1e-06


def mix_kernel(fields_ref, bracket_ref, fraction_ref, out_ref):
    levels = fields_ref.shape[1]
    lev_dev, rows, blocks, cols = out_ref.shape
    plev_dev = rows // F
    lower = bracket_ref[...] - lax.axis_index("lev") * levels
    up = fraction_ref[...]
    down = 1.0 - up
    acc = [jnp.zeros(up.shape, jnp.float32) for _ in range(F)]
    for k in range(levels):
        coef = jnp.where(lower == k, down, jnp.where(lower == k - 1, up, 0.0))
        for f in range(F):
            acc[f] = acc[f] + coef * fields_ref[f, k : k + 1, :].astype(jnp.float32)
    for f in range(F):
        for p in range(lev_dev * plev_dev):
            for s in range(blocks):
                out_ref[p // plev_dev, f * plev_dev + p % plev_dev, s : s + 1, :] = acc[f][
                    p : p + 1, s * cols : (s + 1) * cols
                ]


def count_kernel(intersections_ref, owner_ref, out_ref):
    rows, pairs = out_ref.shape
    entries = intersections_ref.shape[1]
    tile_rows, lanes = owner_ref.shape
    blocks = 8
    tile_dev = 8
    me = lax.axis_index("col")
    col_count = tile_rows * lanes // tile_dev
    eye = lax.broadcasted_iota(jnp.int32, (entries, entries), 0) == lax.broadcasted_iota(
        jnp.int32, (entries, entries), 1
    )

    def column(row):
        return jnp.sum(jnp.where(eye, row, 0.0), axis=1, keepdims=True)

    def lane_row(col):
        return jnp.sum(jnp.where(eye, col, 0.0), axis=0, keepdims=True)

    table = intersections_ref[...].astype(jnp.float32)
    source = column(table[0:1])
    target = column(table[1:2])
    weight = column(table[2:3])
    owner = owner_ref[...].astype(jnp.float32)
    lane = lax.broadcasted_iota(jnp.int32, (entries, lanes), 1).astype(jnp.float32)
    found = jnp.zeros((entries, lanes), jnp.float32)
    for r in range(tile_rows):
        found = found + jnp.where(target == lane + float(r * lanes), owner[r : r + 1], 0.0)
    slot = jnp.sum(found, axis=1, keepdims=True)
    slot = lane_row(slot).astype(jnp.int32)
    dev = slot // tile_dev
    local = slot % tile_dev
    far = dev == (me + col_count // 2) % col_count
    same = dev // GROUP == me // GROUP
    block = jnp.where(same, dev % GROUP, jnp.where(far, GROUP + CROSS, GROUP + dev % CROSS))
    row = block * tile_dev + local
    rows_hit = lax.broadcasted_iota(jnp.int32, (rows, entries), 0) == row
    pair = weight * float(blocks) + source
    pair_hit = lax.broadcasted_iota(jnp.int32, (entries, pairs), 1).astype(jnp.float32) == pair
    out_ref[...] = jnp.dot(
        jnp.where(rows_hit, 1.0, 0.0).astype(jnp.bfloat16),
        jnp.where(pair_hit, 1.0, 0.0).astype(jnp.bfloat16),
        preferred_element_type=jnp.float32,
    )


def remap_kernel(mixed_ref, weights_ref, counts_ref, group_ref, cross_ref, far_ref, parts_ref):
    lev_dev, rows, blocks, cols = mixed_ref.shape
    cells = weights_ref.shape[2]
    interp = mixed_ref[0]
    for k in range(1, lev_dev):
        interp = interp + mixed_ref[k]
    interp = interp.reshape(rows * blocks, cols).astype(jnp.bfloat16)
    for w in range(weights_ref.shape[0]):
        part = jnp.dot(interp, weights_ref[w], preferred_element_type=jnp.float32)
        for r in range(rows):
            parts_ref[w * blocks : (w + 1) * blocks, r * cells : (r + 1) * cells] = part[
                r * blocks : (r + 1) * blocks
            ]
    counts = counts_ref[...].astype(jnp.bfloat16)
    parts = parts_ref[...]
    high = parts.astype(jnp.bfloat16)
    rest = parts - high.astype(jnp.float32)
    middle = rest.astype(jnp.bfloat16)
    low = (rest - middle.astype(jnp.float32)).astype(jnp.bfloat16)
    total = (
        jnp.dot(counts, low, preferred_element_type=jnp.float32)
        + jnp.dot(counts, middle, preferred_element_type=jnp.float32)
        + jnp.dot(counts, high, preferred_element_type=jnp.float32)
    )
    n_group = group_ref.shape[0]
    n_cross = cross_ref.shape[0]
    group_ref[...] = total[:n_group]
    cross_ref[...] = total[n_group : n_group + n_cross]
    far_ref[...] = total[n_group + n_cross :]


def join_kernel(group_ref, cross_ref, out_ref):
    half = cross_ref.shape[0]
    upper = (lax.axis_index("col") % GROUP) >= CROSS
    cross = cross_ref[...]
    out_ref[:half] = group_ref[:half] + jnp.where(upper, 0.0, cross)
    out_ref[half:] = group_ref[half:] + jnp.where(upper, cross, 0.0)


def filter_kernel(near_ref, far_ref, filtered_ref, stats_ref):
    tile_dev = far_ref.shape[0]
    rows = filtered_ref.shape[0]
    cells = filtered_ref.shape[2]
    total = far_ref[...]
    for k in range(near_ref.shape[0] // tile_dev):
        total = total + near_ref[k * tile_dev : (k + 1) * tile_dev]
    lane = lax.broadcasted_iota(jnp.int32, (1, cells), 1)
    stats = jnp.zeros((1, cells), jnp.float32)
    for r in range(rows):
        x = total[:, r * cells : (r + 1) * cells]
        left = jnp.concatenate([x[:, :1], x[:, :-1]], axis=1)
        right = jnp.concatenate([x[:, 1:], x[:, -1:]], axis=1)
        y = 0.25 * left + 0.5 * x + 0.25 * right
        filtered_ref[r] = y
        mean = jnp.sum(jnp.sum(y, axis=0, keepdims=True), axis=1, keepdims=True) / float(tile_dev * cells)
        off = y - mean
        spread = jnp.sum(jnp.sum(off * off, axis=0, keepdims=True), axis=1, keepdims=True)
        stats = jnp.where(lane == r, mean, jnp.where(lane == rows + r, spread, stats))
    stats_ref[...] = jnp.broadcast_to(stats[None], stats_ref.shape)


def per_device(fields, bracket, fraction, remap_weights, intersections, tile_owner):
    lev_dev = lax.axis_size("lev")
    col_count = lax.axis_size("col")
    plev_dev = PLEV // lev_dev
    weights_dev, block_cols, tile_cells = remap_weights.shape
    blocks = fields.shape[2] // block_cols
    tile_dev = tile_owner.shape[0] // col_count
    rows = F * plev_dev
    f32 = jnp.float32

    mixed = pl.pallas_call(
        mix_kernel,
        out_shape=jax.ShapeDtypeStruct((lev_dev, rows, blocks, block_cols), f32),
        name="mix_levels",
    )(fields, bracket, fraction)
    mixed = lax.all_to_all(mixed, "lev", 0, 0, tiled=True)

    n_group = GROUP * tile_dev
    n_cross = CROSS * tile_dev
    counts = pl.pallas_call(
        count_kernel,
        out_shape=jax.ShapeDtypeStruct((n_group + n_cross + tile_dev, weights_dev * blocks), f32),
        name="count_entries",
    )(intersections, tile_owner.reshape(-1, 128))
    group, cross, far = pl.pallas_call(
        remap_kernel,
        out_shape=[
            jax.ShapeDtypeStruct((n, rows * tile_cells), f32) for n in (n_group, n_cross, tile_dev)
        ],
        scratch_shapes=[pltpu.VMEM((weights_dev * blocks, rows * tile_cells), f32)],
        name="remap_blocks",
    )(mixed, remap_weights, counts)

    swap = [
        (d, (d - CROSS) % col_count if d % GROUP < CROSS else (d + CROSS) % col_count)
        for d in range(col_count)
    ]
    opposite = [(d, (d + col_count // 2) % col_count) for d in range(col_count)]
    groups = [[g * GROUP + k for k in range(GROUP)] for g in range(col_count // GROUP)]
    far = lax.ppermute(far, "col", opposite)
    cross = lax.ppermute(cross, "col", swap)
    near = pl.pallas_call(
        join_kernel,
        out_shape=jax.ShapeDtypeStruct((n_group, rows * tile_cells), f32),
        name="join_forwarded",
    )(group, cross)
    near = lax.all_to_all(near, "col", 0, 0, tiled=True, axis_index_groups=groups)

    filtered, stats = pl.pallas_call(
        filter_kernel,
        out_shape=[
            jax.ShapeDtypeStruct((rows, tile_dev, tile_cells), f32),
            jax.ShapeDtypeStruct((col_count, 1, tile_cells), f32),
        ],
        name="filter_tiles",
    )(near, far)
    stats = lax.all_to_all(stats, "col", 0, 0, tiled=True)[:, 0]
    count = float(tile_dev * tile_cells)
    field_mean = jnp.sum(stats[:, :rows], axis=0) / float(col_count)
    apart = stats[:, :rows] - field_mean[None]
    spread = jnp.sum(stats[:, rows : 2 * rows] + count * apart * apart, axis=0)
    field_var = spread / (count * col_count)
    scale = lax.rsqrt(field_var + epsilon)
    normalized = (filtered - field_mean[:, None, None]) * scale[:, None, None]
    return normalized.reshape(F, plev_dev, tile_dev, tile_cells)


def solution(mesh):
    in_specs = (
        P(None, "lev", "col"),
        P(None, "col"),
        P(None, "col"),
        P("col", None, None),
        P(None, "col"),
        P(),
    )
    out_specs = P(None, "lev", "col", None)
    return jax.shard_map(
        per_device, mesh=mesh, in_specs=in_specs, out_specs=out_specs, check_vma=False
    )
```

```python
import jax
import jax.numpy as jnp
from jax import lax
from jax.experimental import pallas as pl
from jax.experimental.pallas import tpu as pltpu
from jax.sharding import PartitionSpec as P


F = 2
PLEV = 8
GROUP = 4
CROSS = 2

epsilon = 1e-06

PARAMS = pltpu.CompilerParams(vmem_limit_bytes=4 << 20)


def mix_levels(fields_ref, bracket_ref, fraction_ref, out_ref):
    levels = fields_ref.shape[1]
    lev_dev, rows, blocks, cols = out_ref.shape
    plev_dev = rows // F
    lower = bracket_ref[...] - lax.axis_index("lev") * levels
    up = fraction_ref[...]
    down = 1.0 - up
    acc = [jnp.zeros(up.shape, jnp.float32) for _ in range(F)]
    for k in range(levels):
        coef = jnp.where(lower == k, down, jnp.where(lower == k - 1, up, 0.0))
        for f in range(F):
            acc[f] = acc[f] + coef * fields_ref[f, k : k + 1, :].astype(jnp.float32)
    for f in range(F):
        for p in range(lev_dev * plev_dev):
            for s in range(blocks):
                out_ref[p // plev_dev, f * plev_dev + p % plev_dev, s : s + 1, :] = acc[f][
                    p : p + 1, s * cols : (s + 1) * cols
                ]


def count_entries(intersections_ref, owner_ref, out_ref):
    rows, pairs = out_ref.shape
    entries = intersections_ref.shape[1]
    tile_rows, lanes = owner_ref.shape
    blocks = 8
    tile_dev = 8
    me = lax.axis_index("col")
    col_count = tile_rows * lanes // tile_dev
    eye = lax.broadcasted_iota(jnp.int32, (entries, entries), 0) == lax.broadcasted_iota(
        jnp.int32, (entries, entries), 1
    )

    def column(row):
        return jnp.sum(jnp.where(eye, row, 0.0), axis=1, keepdims=True)

    def lane_row(col):
        return jnp.sum(jnp.where(eye, col, 0.0), axis=0, keepdims=True)

    table = intersections_ref[...].astype(jnp.float32)
    source = column(table[0:1])
    target = column(table[1:2])
    weight = column(table[2:3])
    owner = owner_ref[...].astype(jnp.float32)
    lane = lax.broadcasted_iota(jnp.int32, (entries, lanes), 1).astype(jnp.float32)
    found = jnp.zeros((entries, lanes), jnp.float32)
    for r in range(tile_rows):
        found = found + jnp.where(target == lane + float(r * lanes), owner[r : r + 1], 0.0)
    slot = jnp.sum(found, axis=1, keepdims=True)
    slot = lane_row(slot).astype(jnp.int32)
    dev = slot // tile_dev
    local = slot % tile_dev
    far = dev == (me + col_count // 2) % col_count
    same = dev // GROUP == me // GROUP
    block = jnp.where(same, dev % GROUP, jnp.where(far, GROUP + CROSS, GROUP + dev % CROSS))
    row = block * tile_dev + local
    rows_hit = lax.broadcasted_iota(jnp.int32, (rows, entries), 0) == row
    pair = weight * float(blocks) + source
    pair_hit = lax.broadcasted_iota(jnp.int32, (entries, pairs), 1).astype(jnp.float32) == pair
    out_ref[...] = jnp.dot(
        jnp.where(rows_hit, 1.0, 0.0).astype(jnp.bfloat16),
        jnp.where(pair_hit, 1.0, 0.0).astype(jnp.bfloat16),
        preferred_element_type=jnp.float32,
    )


def prepare_kernel(
    fields_hbm,
    bracket_hbm,
    fraction_hbm,
    intersections_hbm,
    owner_hbm,
    weights_hbm,
    mixed_ref,
    counts_ref,
    weights_ref,
    fields_ref,
    bracket_ref,
    fraction_ref,
    intersections_ref,
    owner_ref,
    sems,
):
    loads = [
        pltpu.make_async_copy(source, target, sems.at[i])
        for i, (source, target) in enumerate(
            (
                (fields_hbm, fields_ref),
                (bracket_hbm, bracket_ref),
                (fraction_hbm, fraction_ref),
                (intersections_hbm, intersections_ref),
                (owner_hbm, owner_ref),
                (weights_hbm, weights_ref),
            )
        )
    ]
    for load in loads:
        load.start()
    for load in loads[:5]:
        load.wait()
    count_entries(intersections_ref, owner_ref, counts_ref)
    mix_levels(fields_ref, bracket_ref, fraction_ref, mixed_ref)
    loads[5].wait()


def remap_kernel(mixed_ref, weights_ref, counts_ref, group_ref, cross_ref, far_ref, parts_ref):
    lev_dev, rows, blocks, cols = mixed_ref.shape
    cells = weights_ref.shape[2]
    interp = mixed_ref[0]
    for k in range(1, lev_dev):
        interp = interp + mixed_ref[k]
    interp = interp.reshape(rows * blocks, cols).astype(jnp.bfloat16)
    for w in range(weights_ref.shape[0]):
        part = jnp.dot(interp, weights_ref[w], preferred_element_type=jnp.float32)
        for r in range(rows):
            parts_ref[w * blocks : (w + 1) * blocks, r * cells : (r + 1) * cells] = part[
                r * blocks : (r + 1) * blocks
            ]
    counts = counts_ref[...].astype(jnp.bfloat16)
    parts = parts_ref[...]
    high = parts.astype(jnp.bfloat16)
    rest = parts - high.astype(jnp.float32)
    middle = rest.astype(jnp.bfloat16)
    low = (rest - middle.astype(jnp.float32)).astype(jnp.bfloat16)
    total = (
        jnp.dot(counts, low, preferred_element_type=jnp.float32)
        + jnp.dot(counts, middle, preferred_element_type=jnp.float32)
        + jnp.dot(counts, high, preferred_element_type=jnp.float32)
    )
    n_group = group_ref.shape[0]
    n_cross = cross_ref.shape[0]
    group_ref[...] = total[:n_group]
    cross_ref[...] = total[n_group : n_group + n_cross]
    far_ref[...] = total[n_group + n_cross :]


def filter_kernel(near_ref, far_ref, filtered_ref, stats_ref):
    tile_dev = far_ref.shape[0]
    rows = filtered_ref.shape[0]
    cells = filtered_ref.shape[2]
    total = far_ref[...]
    for k in range(near_ref.shape[0] // tile_dev):
        total = total + near_ref[k * tile_dev : (k + 1) * tile_dev]
    lane = lax.broadcasted_iota(jnp.int32, (1, cells), 1)
    stats = jnp.zeros((1, cells), jnp.float32)
    for r in range(rows):
        x = total[:, r * cells : (r + 1) * cells]
        left = jnp.concatenate([x[:, :1], x[:, :-1]], axis=1)
        right = jnp.concatenate([x[:, 1:], x[:, -1:]], axis=1)
        y = 0.25 * left + 0.5 * x + 0.25 * right
        filtered_ref[r] = y
        mean = jnp.sum(jnp.sum(y, axis=0, keepdims=True), axis=1, keepdims=True) / float(tile_dev * cells)
        off = y - mean
        spread = jnp.sum(jnp.sum(off * off, axis=0, keepdims=True), axis=1, keepdims=True)
        stats = jnp.where(lane == r, mean, jnp.where(lane == rows + r, spread, stats))
    stats_ref[...] = jnp.broadcast_to(stats[None], stats_ref.shape)


def remap_step(fields, bracket, fraction, remap_weights, intersections, tile_owner):
    lev_dev = lax.axis_size("lev")
    col_count = lax.axis_size("col")
    plev_dev = PLEV // lev_dev
    weights_dev, block_cols, tile_cells = remap_weights.shape
    blocks = fields.shape[2] // block_cols
    tile_dev = tile_owner.shape[0] // col_count
    rows = F * plev_dev
    f32 = jnp.float32

    n_group = GROUP * tile_dev
    n_cross = CROSS * tile_dev
    owner = tile_owner.reshape(-1, 128)
    sources = (fields, bracket, fraction, intersections, owner, remap_weights)
    anywhere = pl.BlockSpec(memory_space=pltpu.HBM)
    mixed, counts, weights = pl.pallas_call(
        prepare_kernel,
        in_specs=[anywhere] * 6,
        out_shape=[
            jax.ShapeDtypeStruct((lev_dev, rows, blocks, block_cols), f32),
            jax.ShapeDtypeStruct((n_group + n_cross + tile_dev, weights_dev * blocks), f32),
            jax.ShapeDtypeStruct(remap_weights.shape, remap_weights.dtype),
        ],
        scratch_shapes=[
            pltpu.VMEM(fields.shape, fields.dtype),
            pltpu.VMEM(bracket.shape, bracket.dtype),
            pltpu.VMEM(fraction.shape, fraction.dtype),
            pltpu.VMEM(intersections.shape, intersections.dtype),
            pltpu.VMEM(owner.shape, owner.dtype),
            pltpu.SemaphoreType.DMA((6,)),
        ],
        name="mix_and_count",
        compiler_params=PARAMS,
    )(*[pltpu.with_memory_space_constraint(x, pltpu.HBM) for x in sources])
    mixed = lax.all_to_all(mixed, "lev", 0, 0, tiled=True)

    group, cross, far = pl.pallas_call(
        remap_kernel,
        out_shape=[
            jax.ShapeDtypeStruct((n, rows * tile_cells), f32) for n in (n_group, n_cross, tile_dev)
        ],
        scratch_shapes=[pltpu.VMEM((weights_dev * blocks, rows * tile_cells), f32)],
        name="remap_blocks",
        compiler_params=PARAMS,
    )(mixed, weights, counts)

    swap = [
        (d, (d - CROSS) % col_count if d % GROUP < CROSS else (d + CROSS) % col_count)
        for d in range(col_count)
    ]
    opposite = [(d, (d + col_count // 2) % col_count) for d in range(col_count)]
    groups = [[g * GROUP + k for k in range(GROUP)] for g in range(col_count // GROUP)]
    far = lax.ppermute(far, "col", opposite)
    cross = lax.ppermute(cross, "col", swap)
    upper = lax.axis_index("col") % GROUP >= CROSS
    near = group + jnp.concatenate([jnp.where(upper, 0.0, cross), jnp.where(upper, cross, 0.0)])
    near = lax.all_to_all(near, "col", 0, 0, tiled=True, axis_index_groups=groups)

    filtered, stats = pl.pallas_call(
        filter_kernel,
        out_shape=[
            jax.ShapeDtypeStruct((rows, tile_dev, tile_cells), f32),
            jax.ShapeDtypeStruct((col_count, 1, tile_cells), f32),
        ],
        name="filter_tiles",
        compiler_params=PARAMS,
    )(near, far)
    stats = lax.all_to_all(stats, "col", 0, 0, tiled=True)[:, 0]
    count = float(tile_dev * tile_cells)
    field_mean = jnp.sum(stats[:, :rows], axis=0) / float(col_count)
    apart = stats[:, :rows] - field_mean[None]
    spread = jnp.sum(stats[:, rows : 2 * rows] + count * apart * apart, axis=0)
    field_var = spread / (count * col_count)
    scale = lax.rsqrt(field_var + epsilon)
    normalized = (filtered - field_mean[:, None, None]) * scale[:, None, None]
    return normalized.reshape(F, plev_dev, tile_dev, tile_cells)


def solution(mesh):
    in_specs = (
        P(None, "lev", "col"),
        P(None, "col"),
        P(None, "col"),
        P("col", None, None),
        P(None, "col"),
        P(),
    )
    out_specs = P(None, "lev", "col", None)
    return jax.shard_map(
        remap_step, mesh=mesh, in_specs=in_specs, out_specs=out_specs, check_vma=False
    )
```

```python
import jax
import jax.numpy as jnp
from jax import lax
from jax.experimental import pallas as pl
from jax.experimental.pallas import tpu as pltpu
from jax.sharding import PartitionSpec as P


F = 2
PLEV = 8
GROUP = 4
CROSS = 2
ROW = 16
EARLY = 2

epsilon = 1e-06

PARAMS = pltpu.CompilerParams(vmem_limit_bytes=4 << 20)


def mix_levels(fields_ref, bracket_ref, fraction_ref, out_ref):
    levels = fields_ref.shape[1]
    lev_dev, rows, blocks, cols = out_ref.shape
    plev_dev = rows // F
    lower = bracket_ref[...] - lax.axis_index("lev") * levels
    up = fraction_ref[...]
    down = 1.0 - up
    acc = [jnp.zeros(up.shape, jnp.float32) for _ in range(F)]
    for k in range(levels):
        coef = jnp.where(lower == k, down, jnp.where(lower == k - 1, up, 0.0))
        for f in range(F):
            acc[f] = acc[f] + coef * fields_ref[f, k : k + 1, :].astype(jnp.float32)
    for f in range(F):
        for p in range(lev_dev * plev_dev):
            for s in range(blocks):
                out_ref[p // plev_dev, f * plev_dev + p % plev_dev, s : s + 1, :] = acc[f][
                    p : p + 1, s * cols : (s + 1) * cols
                ]


def count_entries(intersections_ref, owner_ref, out_ref):
    rows, pairs = out_ref.shape
    entries = intersections_ref.shape[1]
    tile_rows, lanes = owner_ref.shape
    blocks = 8
    tile_dev = 8
    me = lax.axis_index("col")
    col_count = tile_rows * lanes // tile_dev
    eye = lax.broadcasted_iota(jnp.int32, (entries, entries), 0) == lax.broadcasted_iota(
        jnp.int32, (entries, entries), 1
    )

    def column(row):
        return jnp.sum(jnp.where(eye, row, 0.0), axis=1, keepdims=True)

    def lane_row(col):
        return jnp.sum(jnp.where(eye, col, 0.0), axis=0, keepdims=True)

    table = intersections_ref[...].astype(jnp.float32)
    source = column(table[0:1])
    target = column(table[1:2])
    weight = column(table[2:3])
    owner = owner_ref[...].astype(jnp.float32)
    lane = lax.broadcasted_iota(jnp.int32, (entries, lanes), 1).astype(jnp.float32)
    found = jnp.zeros((entries, lanes), jnp.float32)
    for r in range(tile_rows):
        found = found + jnp.where(target == lane + float(r * lanes), owner[r : r + 1], 0.0)
    slot = jnp.sum(found, axis=1, keepdims=True)
    slot = lane_row(slot).astype(jnp.int32)
    dev = slot // tile_dev
    local = slot % tile_dev
    far = dev == (me + col_count // 2) % col_count
    same = dev // GROUP == me // GROUP
    block = jnp.where(same, dev % GROUP, jnp.where(far, GROUP + CROSS, GROUP + dev % CROSS))
    row = block * tile_dev + local
    rows_hit = lax.broadcasted_iota(jnp.int32, (rows, entries), 0) == row
    pair = weight * float(blocks) + source
    pair_hit = lax.broadcasted_iota(jnp.int32, (entries, pairs), 1).astype(jnp.float32) == pair
    out_ref[...] = jnp.dot(
        jnp.where(rows_hit, 1.0, 0.0).astype(jnp.bfloat16),
        jnp.where(pair_hit, 1.0, 0.0).astype(jnp.bfloat16),
        preferred_element_type=jnp.float32,
    )


def prepare_kernel(
    fields_hbm,
    bracket_hbm,
    fraction_hbm,
    intersections_hbm,
    owner_hbm,
    weights_hbm,
    mixed_ref,
    counts_ref,
    weights_ref,
    fields_ref,
    bracket_ref,
    fraction_ref,
    intersections_ref,
    owner_ref,
    sems,
):
    loads = [
        pltpu.make_async_copy(source, target, sems.at[i])
        for i, (source, target) in enumerate(
            (
                (fields_hbm, fields_ref),
                (bracket_hbm, bracket_ref),
                (fraction_hbm, fraction_ref),
                (intersections_hbm, intersections_ref),
                (owner_hbm, owner_ref),
                (weights_hbm, weights_ref),
            )
        )
    ]
    for load in loads:
        load.start()
    for load in loads[:5]:
        load.wait()
    count_entries(intersections_ref, owner_ref, counts_ref)
    mix_levels(fields_ref, bracket_ref, fraction_ref, mixed_ref)
    loads[5].wait()


def remap_kernel(mixed_ref, weights_ref, counts_ref, group_ref, cross_ref, far_ref, parts_ref):
    lev_dev, rows, blocks, cols = mixed_ref.shape
    cells = weights_ref.shape[2]
    interp = mixed_ref[0]
    for k in range(1, lev_dev):
        interp = interp + mixed_ref[k]
    interp = interp.reshape(rows * blocks, cols).astype(jnp.bfloat16)
    for w in range(weights_ref.shape[0]):
        part = jnp.dot(interp, weights_ref[w], preferred_element_type=jnp.float32)
        for r in range(rows):
            parts_ref[w * blocks : (w + 1) * blocks, r * cells : (r + 1) * cells] = part[
                r * blocks : (r + 1) * blocks
            ]
    counts = counts_ref[...].astype(jnp.bfloat16)
    parts = parts_ref[...]
    high = parts.astype(jnp.bfloat16)
    rest = parts - high.astype(jnp.float32)
    middle = rest.astype(jnp.bfloat16)
    low = (rest - middle.astype(jnp.float32)).astype(jnp.bfloat16)
    total = (
        jnp.dot(counts, low, preferred_element_type=jnp.float32)
        + jnp.dot(counts, middle, preferred_element_type=jnp.float32)
        + jnp.dot(counts, high, preferred_element_type=jnp.float32)
    )
    n_group = group_ref.shape[0]
    n_cross = cross_ref.shape[0]
    group_ref[...] = total[:n_group]
    cross_ref[...] = total[n_group : n_group + n_cross]
    far_ref[...] = total[n_group + n_cross :]


def filter_kernel(near_ref, far_ref, late_ref, filtered_ref, stats_ref):
    tile_dev = far_ref.shape[0]
    rows = filtered_ref.shape[0]
    cells = filtered_ref.shape[2]
    total = far_ref[...] + late_ref[...]
    for k in range(near_ref.shape[0] // tile_dev):
        total = total + near_ref[k * tile_dev : (k + 1) * tile_dev]
    lane = lax.broadcasted_iota(jnp.int32, (1, cells), 1)
    stats = jnp.zeros((1, cells), jnp.float32)
    for r in range(rows):
        x = total[:, r * cells : (r + 1) * cells]
        left = jnp.concatenate([x[:, :1], x[:, :-1]], axis=1)
        right = jnp.concatenate([x[:, 1:], x[:, -1:]], axis=1)
        y = 0.25 * left + 0.5 * x + 0.25 * right
        filtered_ref[r] = y
        mean = jnp.sum(jnp.sum(y, axis=0, keepdims=True), axis=1, keepdims=True) / float(tile_dev * cells)
        off = y - mean
        spread = jnp.sum(jnp.sum(off * off, axis=0, keepdims=True), axis=1, keepdims=True)
        stats = jnp.where(lane == r, mean, jnp.where(lane == rows + r, spread, stats))
    stats_ref[...] = jnp.broadcast_to(stats[None], stats_ref.shape)


def remap_step(fields, bracket, fraction, remap_weights, intersections, tile_owner):
    lev_dev = lax.axis_size("lev")
    col_count = lax.axis_size("col")
    plev_dev = PLEV // lev_dev
    weights_dev, block_cols, tile_cells = remap_weights.shape
    blocks = fields.shape[2] // block_cols
    tile_dev = tile_owner.shape[0] // col_count
    rows = F * plev_dev
    f32 = jnp.float32

    n_group = GROUP * tile_dev
    n_cross = CROSS * tile_dev
    owner = tile_owner.reshape(-1, 128)
    sources = (fields, bracket, fraction, intersections, owner, remap_weights)
    anywhere = pl.BlockSpec(memory_space=pltpu.HBM)
    mixed, counts, weights = pl.pallas_call(
        prepare_kernel,
        in_specs=[anywhere] * 6,
        out_shape=[
            jax.ShapeDtypeStruct((lev_dev, rows, blocks, block_cols), f32),
            jax.ShapeDtypeStruct((n_group + n_cross + tile_dev, weights_dev * blocks), f32),
            jax.ShapeDtypeStruct(remap_weights.shape, remap_weights.dtype),
        ],
        scratch_shapes=[
            pltpu.VMEM(fields.shape, fields.dtype),
            pltpu.VMEM(bracket.shape, bracket.dtype),
            pltpu.VMEM(fraction.shape, fraction.dtype),
            pltpu.VMEM(intersections.shape, intersections.dtype),
            pltpu.VMEM(owner.shape, owner.dtype),
            pltpu.SemaphoreType.DMA((6,)),
        ],
        name="mix_and_count",
        compiler_params=PARAMS,
    )(*[pltpu.with_memory_space_constraint(x, pltpu.HBM) for x in sources])
    mixed = lax.all_to_all(mixed, "lev", 0, 0, tiled=True)

    group, cross, far = pl.pallas_call(
        remap_kernel,
        out_shape=[
            jax.ShapeDtypeStruct((n, rows * tile_cells), f32) for n in (n_group, n_cross, tile_dev)
        ],
        scratch_shapes=[pltpu.VMEM((weights_dev * blocks, rows * tile_cells), f32)],
        name="remap_blocks",
        compiler_params=PARAMS,
    )(mixed, weights, counts)

    swap = [
        (d, (d - CROSS) % col_count if d % GROUP < CROSS else (d + CROSS) % col_count)
        for d in range(col_count)
    ]
    opposite = [(d, (d + col_count // 2) % col_count) for d in range(col_count)]
    early = [pair for pair in opposite if pair[0] % ROW < EARLY]
    late = [pair for pair in opposite if pair[0] % ROW >= EARLY]
    groups = [[g * GROUP + k for k in range(GROUP)] for g in range(col_count // GROUP)]
    far_a = lax.ppermute(far, "col", early)
    far_b = lax.ppermute(far, "col", late)
    cross = lax.ppermute(cross, "col", swap)
    upper = lax.axis_index("col") % GROUP >= CROSS
    near = group + jnp.concatenate([jnp.where(upper, 0.0, cross), jnp.where(upper, cross, 0.0)])
    near = lax.all_to_all(near, "col", 0, 0, tiled=True, axis_index_groups=groups)

    filtered, stats = pl.pallas_call(
        filter_kernel,
        out_shape=[
            jax.ShapeDtypeStruct((rows, tile_dev, tile_cells), f32),
            jax.ShapeDtypeStruct((col_count, 1, tile_cells), f32),
        ],
        name="filter_tiles",
        compiler_params=PARAMS,
    )(near, far_a, far_b)
    lead = 72
    order = [(lead + k) % col_count for k in range(col_count)]
    stats = lax.all_to_all(stats, "col", 0, 0, tiled=True, axis_index_groups=[order])[:, 0]
    count = float(tile_dev * tile_cells)
    field_mean = jnp.sum(stats[:, :rows], axis=0) / float(col_count)
    apart = stats[:, :rows] - field_mean[None]
    spread = jnp.sum(stats[:, rows : 2 * rows] + count * apart * apart, axis=0)
    field_var = spread / (count * col_count)
    scale = lax.rsqrt(field_var + epsilon)
    normalized = (filtered - field_mean[:, None, None]) * scale[:, None, None]
    return normalized.reshape(F, plev_dev, tile_dev, tile_cells)


def solution(mesh):
    in_specs = (
        P(None, "lev", "col"),
        P(None, "col"),
        P(None, "col"),
        P("col", None, None),
        P(None, "col"),
        P(),
    )
    out_specs = P(None, "lev", "col", None)
    return jax.shard_map(
        remap_step, mesh=mesh, in_specs=in_specs, out_specs=out_specs, check_vma=False
    )
```

```python
import jax
import jax.numpy as jnp
from jax import lax
from jax.experimental import pallas as pl
from jax.experimental.pallas import tpu as pltpu
from jax.sharding import PartitionSpec as P


F = 2
PLEV = 8
GROUP = 4
CROSS = 2
ROW = 16
EARLY = 2
LEV_FIRST = 2
NEAR_FIRST = 3
STATS_FIRST = 89

epsilon = 1e-06

PARAMS = pltpu.CompilerParams(vmem_limit_bytes=4 << 20)


def mix_levels(fields_ref, bracket_ref, fraction_ref, out_ref):
    levels = fields_ref.shape[1]
    lev_dev, rows, blocks, cols = out_ref.shape
    plev_dev = rows // F
    lower = bracket_ref[...] - lax.axis_index("lev") * levels
    up = fraction_ref[...]
    down = 1.0 - up
    acc = [jnp.zeros(up.shape, jnp.float32) for _ in range(F)]
    for k in range(levels):
        coef = jnp.where(lower == k, down, jnp.where(lower == k - 1, up, 0.0))
        for f in range(F):
            acc[f] = acc[f] + coef * fields_ref[f, k : k + 1, :].astype(jnp.float32)
    for f in range(F):
        for p in range(lev_dev * plev_dev):
            for s in range(blocks):
                out_ref[(p // plev_dev - LEV_FIRST) % lev_dev, f * plev_dev + p % plev_dev, s : s + 1, :] = acc[f][
                    p : p + 1, s * cols : (s + 1) * cols
                ]


def count_entries(intersections_ref, owner_ref, out_ref):
    rows, pairs = out_ref.shape
    entries = intersections_ref.shape[1]
    tile_rows, lanes = owner_ref.shape
    blocks = 8
    tile_dev = 8
    me = lax.axis_index("col")
    col_count = tile_rows * lanes // tile_dev
    eye = lax.broadcasted_iota(jnp.int32, (entries, entries), 0) == lax.broadcasted_iota(
        jnp.int32, (entries, entries), 1
    )

    def column(row):
        return jnp.sum(jnp.where(eye, row, 0.0), axis=1, keepdims=True)

    def lane_row(col):
        return jnp.sum(jnp.where(eye, col, 0.0), axis=0, keepdims=True)

    table = intersections_ref[...].astype(jnp.float32)
    source = column(table[0:1])
    target = column(table[1:2])
    weight = column(table[2:3])
    owner = owner_ref[...].astype(jnp.float32)
    lane = lax.broadcasted_iota(jnp.int32, (entries, lanes), 1).astype(jnp.float32)
    found = jnp.zeros((entries, lanes), jnp.float32)
    for r in range(tile_rows):
        found = found + jnp.where(target == lane + float(r * lanes), owner[r : r + 1], 0.0)
    slot = jnp.sum(found, axis=1, keepdims=True)
    slot = lane_row(slot).astype(jnp.int32)
    dev = slot // tile_dev
    local = slot % tile_dev
    far = dev == (me + col_count // 2) % col_count
    same = dev // GROUP == me // GROUP
    block = jnp.where(same, (dev + GROUP - NEAR_FIRST) % GROUP, jnp.where(far, GROUP + CROSS, GROUP + dev % CROSS))
    row = block * tile_dev + local
    rows_hit = lax.broadcasted_iota(jnp.int32, (rows, entries), 0) == row
    pair = weight * float(blocks) + source
    pair_hit = lax.broadcasted_iota(jnp.int32, (entries, pairs), 1).astype(jnp.float32) == pair
    out_ref[...] = jnp.dot(
        jnp.where(rows_hit, 1.0, 0.0).astype(jnp.bfloat16),
        jnp.where(pair_hit, 1.0, 0.0).astype(jnp.bfloat16),
        preferred_element_type=jnp.float32,
    )


def prepare_kernel(
    fields_hbm,
    bracket_hbm,
    fraction_hbm,
    intersections_hbm,
    owner_hbm,
    weights_hbm,
    mixed_ref,
    counts_ref,
    weights_ref,
    fields_ref,
    bracket_ref,
    fraction_ref,
    intersections_ref,
    owner_ref,
    sems,
):
    loads = [
        pltpu.make_async_copy(source, target, sems.at[i])
        for i, (source, target) in enumerate(
            (
                (fields_hbm, fields_ref),
                (bracket_hbm, bracket_ref),
                (fraction_hbm, fraction_ref),
                (intersections_hbm, intersections_ref),
                (owner_hbm, owner_ref),
                (weights_hbm, weights_ref),
            )
        )
    ]
    for load in loads:
        load.start()
    for load in loads[:5]:
        load.wait()
    count_entries(intersections_ref, owner_ref, counts_ref)
    mix_levels(fields_ref, bracket_ref, fraction_ref, mixed_ref)
    loads[5].wait()


def remap_kernel(mixed_ref, weights_ref, counts_ref, group_ref, cross_ref, far_ref, parts_ref):
    lev_dev, rows, blocks, cols = mixed_ref.shape
    cells = weights_ref.shape[2]
    interp = mixed_ref[0]
    for k in range(1, lev_dev):
        interp = interp + mixed_ref[k]
    interp = interp.reshape(rows * blocks, cols).astype(jnp.bfloat16)
    for w in range(weights_ref.shape[0]):
        part = jnp.dot(interp, weights_ref[w], preferred_element_type=jnp.float32)
        for r in range(rows):
            parts_ref[w * blocks : (w + 1) * blocks, r * cells : (r + 1) * cells] = part[
                r * blocks : (r + 1) * blocks
            ]
    counts = counts_ref[...].astype(jnp.bfloat16)
    parts = parts_ref[...]
    high = parts.astype(jnp.bfloat16)
    rest = parts - high.astype(jnp.float32)
    middle = rest.astype(jnp.bfloat16)
    low = (rest - middle.astype(jnp.float32)).astype(jnp.bfloat16)
    total = (
        jnp.dot(counts, low, preferred_element_type=jnp.float32)
        + jnp.dot(counts, middle, preferred_element_type=jnp.float32)
        + jnp.dot(counts, high, preferred_element_type=jnp.float32)
    )
    n_group = group_ref.shape[0]
    n_cross = cross_ref.shape[0]
    group_ref[...] = total[:n_group]
    cross_ref[...] = total[n_group : n_group + n_cross]
    far_ref[...] = total[n_group + n_cross :]


def join_kernel(group_ref, cross_ref, out_ref):
    tile_dev = cross_ref.shape[0] // CROSS
    upper = lax.axis_index("col") % GROUP >= CROSS
    for i in range(GROUP):
        member = (i + NEAR_FIRST) % GROUP
        mine = upper if member >= CROSS else jnp.logical_not(upper)
        start = member % CROSS * tile_dev
        forwarded = cross_ref[start : start + tile_dev]
        rows = slice(i * tile_dev, (i + 1) * tile_dev)
        out_ref[rows] = group_ref[rows] + jnp.where(mine, forwarded, 0.0)


def filter_kernel(near_ref, far_ref, late_ref, filtered_ref, stats_ref):
    tile_dev = far_ref.shape[0]
    rows = filtered_ref.shape[0]
    cells = filtered_ref.shape[2]
    total = far_ref[...] + late_ref[...]
    for k in range(near_ref.shape[0] // tile_dev):
        total = total + near_ref[k * tile_dev : (k + 1) * tile_dev]
    lane = lax.broadcasted_iota(jnp.int32, (1, cells), 1)
    stats = jnp.zeros((1, cells), jnp.float32)
    for r in range(rows):
        x = total[:, r * cells : (r + 1) * cells]
        left = jnp.concatenate([x[:, :1], x[:, :-1]], axis=1)
        right = jnp.concatenate([x[:, 1:], x[:, -1:]], axis=1)
        y = 0.25 * left + 0.5 * x + 0.25 * right
        filtered_ref[r] = y
        mean = jnp.sum(jnp.sum(y, axis=0, keepdims=True), axis=1, keepdims=True) / float(tile_dev * cells)
        off = y - mean
        spread = jnp.sum(jnp.sum(off * off, axis=0, keepdims=True), axis=1, keepdims=True)
        stats = jnp.where(lane == r, mean, jnp.where(lane == rows + r, spread, stats))
    stats_ref[...] = jnp.broadcast_to(stats[None], stats_ref.shape)


def remap_step(fields, bracket, fraction, remap_weights, intersections, tile_owner):
    lev_dev = lax.axis_size("lev")
    col_count = lax.axis_size("col")
    plev_dev = PLEV // lev_dev
    weights_dev, block_cols, tile_cells = remap_weights.shape
    blocks = fields.shape[2] // block_cols
    tile_dev = tile_owner.shape[0] // col_count
    rows = F * plev_dev
    f32 = jnp.float32

    n_group = GROUP * tile_dev
    n_cross = CROSS * tile_dev
    owner = tile_owner.reshape(-1, 128)
    sources = (fields, bracket, fraction, intersections, owner, remap_weights)
    anywhere = pl.BlockSpec(memory_space=pltpu.HBM)
    mixed, counts, weights = pl.pallas_call(
        prepare_kernel,
        in_specs=[anywhere] * 6,
        out_shape=[
            jax.ShapeDtypeStruct((lev_dev, rows, blocks, block_cols), f32),
            jax.ShapeDtypeStruct((n_group + n_cross + tile_dev, weights_dev * blocks), f32),
            jax.ShapeDtypeStruct(remap_weights.shape, remap_weights.dtype),
        ],
        scratch_shapes=[
            pltpu.VMEM(fields.shape, fields.dtype),
            pltpu.VMEM(bracket.shape, bracket.dtype),
            pltpu.VMEM(fraction.shape, fraction.dtype),
            pltpu.VMEM(intersections.shape, intersections.dtype),
            pltpu.VMEM(owner.shape, owner.dtype),
            pltpu.SemaphoreType.DMA((6,)),
        ],
        name="mix_and_count",
        compiler_params=PARAMS,
    )(*[pltpu.with_memory_space_constraint(x, pltpu.HBM) for x in sources])
    levs = [[(k + LEV_FIRST) % lev_dev for k in range(lev_dev)]]
    mixed = lax.all_to_all(mixed, "lev", 0, 0, tiled=True, axis_index_groups=levs)

    group, cross, far = pl.pallas_call(
        remap_kernel,
        out_shape=[
            jax.ShapeDtypeStruct((n, rows * tile_cells), f32) for n in (n_group, n_cross, tile_dev)
        ],
        scratch_shapes=[pltpu.VMEM((weights_dev * blocks, rows * tile_cells), f32)],
        name="remap_blocks",
        compiler_params=PARAMS,
    )(mixed, weights, counts)

    swap = [
        (d, (d - CROSS) % col_count if d % GROUP < CROSS else (d + CROSS) % col_count)
        for d in range(col_count)
    ]
    opposite = [(d, (d + col_count // 2) % col_count) for d in range(col_count)]
    early = [pair for pair in opposite if pair[0] % ROW < EARLY]
    late = [pair for pair in opposite if pair[0] % ROW >= EARLY]
    groups = [[g * GROUP + (k + NEAR_FIRST) % GROUP for k in range(GROUP)] for g in range(col_count // GROUP)]
    far_a = lax.ppermute(far, "col", early)
    far_b = lax.ppermute(far, "col", late)
    cross = lax.ppermute(cross, "col", swap)
    near = pl.pallas_call(
        join_kernel,
        out_shape=jax.ShapeDtypeStruct((n_group, rows * tile_cells), f32),
        name="join_forwarded",
        compiler_params=PARAMS,
    )(group, cross)
    near = lax.all_to_all(near, "col", 0, 0, tiled=True, axis_index_groups=groups)

    filtered, stats = pl.pallas_call(
        filter_kernel,
        out_shape=[
            jax.ShapeDtypeStruct((rows, tile_dev, tile_cells), f32),
            jax.ShapeDtypeStruct((col_count, 1, tile_cells), f32),
        ],
        name="filter_tiles",
        compiler_params=PARAMS,
    )(near, far_a, far_b)
    lead = STATS_FIRST
    order = sorted(range(col_count), key=lambda d: (d != lead, d % ROW, d))
    stats = lax.all_to_all(stats, "col", 0, 0, tiled=True, axis_index_groups=[order])[:, 0]
    count = float(tile_dev * tile_cells)
    field_mean = jnp.sum(stats[:, :rows], axis=0) / float(col_count)
    apart = stats[:, :rows] - field_mean[None]
    spread = jnp.sum(stats[:, rows : 2 * rows] + count * apart * apart, axis=0)
    field_var = spread / (count * col_count)
    scale = lax.rsqrt(field_var + epsilon)
    normalized = (filtered - field_mean[:, None, None]) * scale[:, None, None]
    return normalized.reshape(F, plev_dev, tile_dev, tile_cells)


def solution(mesh):
    in_specs = (
        P(None, "lev", "col"),
        P(None, "col"),
        P(None, "col"),
        P("col", None, None),
        P(None, "col"),
        P(),
    )
    out_specs = P(None, "lev", "col", None)
    return jax.shard_map(
        remap_step, mesh=mesh, in_specs=in_specs, out_specs=out_specs, check_vma=False
    )
```

```python
import jax
import jax.numpy as jnp
from jax import lax
from jax.experimental import pallas as pl
from jax.experimental.pallas import tpu as pltpu
from jax.sharding import PartitionSpec as P


F = 2
PLEV = 8
GROUP = 4
CROSS = 2
ROW = 16
EARLY = 4
LEV_FIRST = 2
NEAR_FIRST = 3
STATS_FIRST = 89

epsilon = 1e-06

PARAMS = pltpu.CompilerParams(vmem_limit_bytes=4 << 20)


def mix_levels(fields_ref, bracket_ref, fraction_ref, out_ref):
    levels = fields_ref.shape[1]
    lev_dev, rows, blocks, cols = out_ref.shape
    plev_dev = rows // F
    lower = bracket_ref[...] - lax.axis_index("lev") * levels
    up = fraction_ref[...]
    down = 1.0 - up
    acc = [jnp.zeros(up.shape, jnp.float32) for _ in range(F)]
    for k in range(levels):
        coef = jnp.where(lower == k, down, jnp.where(lower == k - 1, up, 0.0))
        for f in range(F):
            acc[f] = acc[f] + coef * fields_ref[f, k : k + 1, :].astype(jnp.float32)
    for f in range(F):
        for p in range(lev_dev * plev_dev):
            for s in range(blocks):
                out_ref[(p // plev_dev - LEV_FIRST) % lev_dev, f * plev_dev + p % plev_dev, s : s + 1, :] = acc[f][
                    p : p + 1, s * cols : (s + 1) * cols
                ]


def count_entries(intersections_ref, owner_ref, out_ref):
    rows, pairs = out_ref.shape
    entries = intersections_ref.shape[1]
    tile_rows, lanes = owner_ref.shape
    blocks = 8
    tile_dev = 8
    me = lax.axis_index("col")
    col_count = tile_rows * lanes // tile_dev
    eye = lax.broadcasted_iota(jnp.int32, (entries, entries), 0) == lax.broadcasted_iota(
        jnp.int32, (entries, entries), 1
    )

    def column(row):
        return jnp.sum(jnp.where(eye, row, 0.0), axis=1, keepdims=True)

    def lane_row(col):
        return jnp.sum(jnp.where(eye, col, 0.0), axis=0, keepdims=True)

    table = intersections_ref[...].astype(jnp.float32)
    source = column(table[0:1])
    target = column(table[1:2])
    weight = column(table[2:3])
    owner = owner_ref[...].astype(jnp.float32)
    lane = lax.broadcasted_iota(jnp.int32, (entries, lanes), 1).astype(jnp.float32)
    found = jnp.zeros((entries, lanes), jnp.float32)
    for r in range(tile_rows):
        found = found + jnp.where(target == lane + float(r * lanes), owner[r : r + 1], 0.0)
    slot = jnp.sum(found, axis=1, keepdims=True)
    slot = lane_row(slot).astype(jnp.int32)
    dev = slot // tile_dev
    local = slot % tile_dev
    far = dev == (me + col_count // 2) % col_count
    same = dev // GROUP == me // GROUP
    block = jnp.where(same, (dev + GROUP - NEAR_FIRST) % GROUP, jnp.where(far, GROUP + CROSS, GROUP + dev % CROSS))
    row = block * tile_dev + local
    rows_hit = lax.broadcasted_iota(jnp.int32, (rows, entries), 0) == row
    pair = weight * float(blocks) + source
    pair_hit = lax.broadcasted_iota(jnp.int32, (entries, pairs), 1).astype(jnp.float32) == pair
    out_ref[...] = jnp.dot(
        jnp.where(rows_hit, 1.0, 0.0).astype(jnp.bfloat16),
        jnp.where(pair_hit, 1.0, 0.0).astype(jnp.bfloat16),
        preferred_element_type=jnp.float32,
    )


def prepare_kernel(
    fields_hbm,
    bracket_hbm,
    fraction_hbm,
    intersections_hbm,
    owner_hbm,
    weights_hbm,
    mixed_ref,
    counts_ref,
    weights_ref,
    fields_ref,
    bracket_ref,
    fraction_ref,
    intersections_ref,
    owner_ref,
    sems,
):
    loads = [
        pltpu.make_async_copy(source, target, sems.at[i])
        for i, (source, target) in enumerate(
            (
                (fields_hbm, fields_ref),
                (bracket_hbm, bracket_ref),
                (fraction_hbm, fraction_ref),
                (intersections_hbm, intersections_ref),
                (owner_hbm, owner_ref),
                (weights_hbm, weights_ref),
            )
        )
    ]
    for load in loads:
        load.start()
    for load in loads[:5]:
        load.wait()
    count_entries(intersections_ref, owner_ref, counts_ref)
    mix_levels(fields_ref, bracket_ref, fraction_ref, mixed_ref)
    loads[5].wait()


def remap_kernel(mixed_ref, weights_ref, counts_ref, group_ref, cross_ref, far_ref, parts_ref):
    lev_dev, rows, blocks, cols = mixed_ref.shape
    cells = weights_ref.shape[2]
    interp = mixed_ref[0]
    for k in range(1, lev_dev):
        interp = interp + mixed_ref[k]
    interp = interp.reshape(rows * blocks, cols).astype(jnp.bfloat16)
    for w in range(weights_ref.shape[0]):
        part = jnp.dot(interp, weights_ref[w], preferred_element_type=jnp.float32)
        for r in range(rows):
            parts_ref[w * blocks : (w + 1) * blocks, r * cells : (r + 1) * cells] = part[
                r * blocks : (r + 1) * blocks
            ]
    counts = counts_ref[...].astype(jnp.bfloat16)
    parts = parts_ref[...]
    high = parts.astype(jnp.bfloat16)
    rest = parts - high.astype(jnp.float32)
    middle = rest.astype(jnp.bfloat16)
    low = (rest - middle.astype(jnp.float32)).astype(jnp.bfloat16)
    total = (
        jnp.dot(counts, low, preferred_element_type=jnp.float32)
        + jnp.dot(counts, middle, preferred_element_type=jnp.float32)
        + jnp.dot(counts, high, preferred_element_type=jnp.float32)
    )
    n_group = group_ref.shape[0]
    n_cross = cross_ref.shape[0]
    group_ref[...] = total[:n_group]
    cross_ref[...] = total[n_group : n_group + n_cross]
    far_ref[...] = total[n_group + n_cross :]


def join_kernel(group_ref, cross_ref, out_ref):
    tile_dev = cross_ref.shape[0] // CROSS
    upper = lax.axis_index("col") % GROUP >= CROSS
    for i in range(GROUP):
        member = (i + NEAR_FIRST) % GROUP
        mine = upper if member >= CROSS else jnp.logical_not(upper)
        start = member % CROSS * tile_dev
        forwarded = cross_ref[start : start + tile_dev]
        rows = slice(i * tile_dev, (i + 1) * tile_dev)
        out_ref[rows] = group_ref[rows] + jnp.where(mine, forwarded, 0.0)


def filter_kernel(near_ref, far_ref, late_ref, filtered_ref, stats_ref):
    tile_dev = far_ref.shape[0]
    rows = filtered_ref.shape[0]
    cells = filtered_ref.shape[2]
    total = far_ref[...] + late_ref[...]
    for k in range(near_ref.shape[0] // tile_dev):
        total = total + near_ref[k * tile_dev : (k + 1) * tile_dev]
    lane = lax.broadcasted_iota(jnp.int32, (1, cells), 1)
    stats = jnp.zeros((1, cells), jnp.float32)
    for r in range(rows):
        x = total[:, r * cells : (r + 1) * cells]
        left = jnp.concatenate([x[:, :1], x[:, :-1]], axis=1)
        right = jnp.concatenate([x[:, 1:], x[:, -1:]], axis=1)
        y = 0.25 * left + 0.5 * x + 0.25 * right
        filtered_ref[r] = y
        mean = jnp.sum(jnp.sum(y, axis=0, keepdims=True), axis=1, keepdims=True) / float(tile_dev * cells)
        off = y - mean
        spread = jnp.sum(jnp.sum(off * off, axis=0, keepdims=True), axis=1, keepdims=True)
        stats = jnp.where(lane == r, mean, jnp.where(lane == rows + r, spread, stats))
    stats_ref[...] = jnp.broadcast_to(stats, stats_ref.shape)


def remap_step(fields, bracket, fraction, remap_weights, intersections, tile_owner):
    lev_dev = lax.axis_size("lev")
    col_count = lax.axis_size("col")
    plev_dev = PLEV // lev_dev
    weights_dev, block_cols, tile_cells = remap_weights.shape
    blocks = fields.shape[2] // block_cols
    tile_dev = tile_owner.shape[0] // col_count
    rows = F * plev_dev
    f32 = jnp.float32

    n_group = GROUP * tile_dev
    n_cross = CROSS * tile_dev
    owner = tile_owner.reshape(-1, 128)
    sources = (fields, bracket, fraction, intersections, owner, remap_weights)
    anywhere = pl.BlockSpec(memory_space=pltpu.HBM)
    mixed, counts, weights = pl.pallas_call(
        prepare_kernel,
        in_specs=[anywhere] * 6,
        out_shape=[
            jax.ShapeDtypeStruct((lev_dev, rows, blocks, block_cols), f32),
            jax.ShapeDtypeStruct((n_group + n_cross + tile_dev, weights_dev * blocks), f32),
            jax.ShapeDtypeStruct(remap_weights.shape, remap_weights.dtype),
        ],
        scratch_shapes=[
            pltpu.VMEM(fields.shape, fields.dtype),
            pltpu.VMEM(bracket.shape, bracket.dtype),
            pltpu.VMEM(fraction.shape, fraction.dtype),
            pltpu.VMEM(intersections.shape, intersections.dtype),
            pltpu.VMEM(owner.shape, owner.dtype),
            pltpu.SemaphoreType.DMA((6,)),
        ],
        name="mix_and_count",
        compiler_params=PARAMS,
    )(*[pltpu.with_memory_space_constraint(x, pltpu.HBM) for x in sources])
    levs = [[(k + LEV_FIRST) % lev_dev for k in range(lev_dev)]]
    mixed = lax.all_to_all(mixed, "lev", 0, 0, tiled=True, axis_index_groups=levs)

    group, cross, far = pl.pallas_call(
        remap_kernel,
        out_shape=[
            jax.ShapeDtypeStruct((n, rows * tile_cells), f32) for n in (n_group, n_cross, tile_dev)
        ],
        scratch_shapes=[pltpu.VMEM((weights_dev * blocks, rows * tile_cells), f32)],
        name="remap_blocks",
        compiler_params=PARAMS,
    )(mixed, weights, counts)

    swap = [
        (d, (d - CROSS) % col_count if d % GROUP < CROSS else (d + CROSS) % col_count)
        for d in range(col_count)
    ]
    opposite = [(d, (d + col_count // 2) % col_count) for d in range(col_count)]
    early = [pair for pair in opposite if pair[0] % ROW < EARLY]
    late = [pair for pair in opposite if pair[0] % ROW >= EARLY]
    groups = [[g * GROUP + (k + NEAR_FIRST) % GROUP for k in range(GROUP)] for g in range(col_count // GROUP)]
    far_a = lax.ppermute(far, "col", early)
    far_b = lax.ppermute(far, "col", late)
    cross = lax.ppermute(cross, "col", swap)
    near = pl.pallas_call(
        join_kernel,
        out_shape=jax.ShapeDtypeStruct((n_group, rows * tile_cells), f32),
        name="join_forwarded",
        compiler_params=PARAMS,
    )(group, cross)
    near = lax.all_to_all(near, "col", 0, 0, tiled=True, axis_index_groups=groups)

    filtered, stats = pl.pallas_call(
        filter_kernel,
        out_shape=[
            jax.ShapeDtypeStruct((rows, tile_dev, tile_cells), f32),
            jax.ShapeDtypeStruct((col_count, tile_cells), f32),
        ],
        name="filter_tiles",
        compiler_params=PARAMS,
    )(near, far_a, far_b)
    lead = STATS_FIRST
    order = sorted(range(col_count), key=lambda d: (d != lead, d % ROW, d))
    stats = stats.reshape(col_count, 1, tile_cells)
    stats = lax.all_to_all(stats, "col", 0, 0, tiled=True, axis_index_groups=[order])[:, 0]
    count = float(tile_dev * tile_cells)
    field_mean = jnp.sum(stats[:, :rows], axis=0) / float(col_count)
    apart = stats[:, :rows] - field_mean[None]
    spread = jnp.sum(stats[:, rows : 2 * rows] + count * apart * apart, axis=0)
    field_var = spread / (count * col_count)
    scale = lax.rsqrt(field_var + epsilon)
    normalized = (filtered - field_mean[:, None, None]) * scale[:, None, None]
    return normalized.reshape(F, plev_dev, tile_dev, tile_cells)


def solution(mesh):
    in_specs = (
        P(None, "lev", "col"),
        P(None, "col"),
        P(None, "col"),
        P("col", None, None),
        P(None, "col"),
        P(),
    )
    out_specs = P(None, "lev", "col", None)
    return jax.shard_map(
        remap_step, mesh=mesh, in_specs=in_specs, out_specs=out_specs, check_vma=False
    )
```

```python
import jax
import jax.numpy as jnp
from jax import lax
from jax.experimental import pallas as pl
from jax.experimental.pallas import tpu as pltpu
from jax.sharding import PartitionSpec as P


F = 2
PLEV = 8
GROUP = 4
CROSS = 2
ROW = 16
EARLY = 2
LEV_FIRST = 2
NEAR_FIRST = 3
STATS_FIRST = 89

epsilon = 1e-06

PARAMS = pltpu.CompilerParams(vmem_limit_bytes=4 << 20)


def mix_levels(fields_ref, bracket_ref, fraction_ref, out_ref):
    levels = fields_ref.shape[1]
    lev_dev, rows, blocks, cols = out_ref.shape
    plev_dev = rows // F
    lower = bracket_ref[...] - lax.axis_index("lev") * levels
    up = fraction_ref[...]
    down = 1.0 - up
    acc = [jnp.zeros(up.shape, jnp.float32) for _ in range(F)]
    for k in range(levels):
        coef = jnp.where(lower == k, down, jnp.where(lower == k - 1, up, 0.0))
        for f in range(F):
            acc[f] = acc[f] + coef * fields_ref[f, k : k + 1, :].astype(jnp.float32)
    for f in range(F):
        for p in range(lev_dev * plev_dev):
            for s in range(blocks):
                out_ref[(p // plev_dev - LEV_FIRST) % lev_dev, f * plev_dev + p % plev_dev, s : s + 1, :] = acc[f][
                    p : p + 1, s * cols : (s + 1) * cols
                ]


def count_entries(intersections_ref, owner_ref, out_ref):
    rows, pairs = out_ref.shape
    entries = intersections_ref.shape[1]
    tile_rows, lanes = owner_ref.shape
    blocks = 8
    tile_dev = 8
    me = lax.axis_index("col")
    col_count = tile_rows * lanes // tile_dev
    eye = lax.broadcasted_iota(jnp.int32, (entries, entries), 0) == lax.broadcasted_iota(
        jnp.int32, (entries, entries), 1
    )

    def column(row):
        return jnp.sum(jnp.where(eye, row, 0.0), axis=1, keepdims=True)

    def lane_row(col):
        return jnp.sum(jnp.where(eye, col, 0.0), axis=0, keepdims=True)

    table = intersections_ref[...].astype(jnp.float32)
    source = column(table[0:1])
    target = column(table[1:2])
    weight = column(table[2:3])
    owner = owner_ref[...].astype(jnp.float32)
    lane = lax.broadcasted_iota(jnp.int32, (entries, lanes), 1).astype(jnp.float32)
    found = jnp.zeros((entries, lanes), jnp.float32)
    for r in range(tile_rows):
        found = found + jnp.where(target == lane + float(r * lanes), owner[r : r + 1], 0.0)
    slot = jnp.sum(found, axis=1, keepdims=True)
    slot = lane_row(slot).astype(jnp.int32)
    dev = slot // tile_dev
    local = slot % tile_dev
    far = dev == (me + col_count // 2) % col_count
    same = dev // GROUP == me // GROUP
    block = jnp.where(same, (dev + GROUP - NEAR_FIRST) % GROUP, jnp.where(far, GROUP + CROSS, GROUP + dev % CROSS))
    row = block * tile_dev + local
    rows_hit = lax.broadcasted_iota(jnp.int32, (rows, entries), 0) == row
    pair = weight * float(blocks) + source
    pair_hit = lax.broadcasted_iota(jnp.int32, (entries, pairs), 1).astype(jnp.float32) == pair
    out_ref[...] = jnp.dot(
        jnp.where(rows_hit, 1.0, 0.0).astype(jnp.bfloat16),
        jnp.where(pair_hit, 1.0, 0.0).astype(jnp.bfloat16),
        preferred_element_type=jnp.float32,
    )


def prepare_kernel(
    fields_hbm,
    bracket_hbm,
    fraction_hbm,
    intersections_hbm,
    owner_hbm,
    weights_hbm,
    mixed_ref,
    counts_ref,
    weights_ref,
    fields_ref,
    bracket_ref,
    fraction_ref,
    intersections_ref,
    owner_ref,
    sems,
):
    loads = [
        pltpu.make_async_copy(source, target, sems.at[i])
        for i, (source, target) in enumerate(
            (
                (fields_hbm, fields_ref),
                (bracket_hbm, bracket_ref),
                (fraction_hbm, fraction_ref),
                (intersections_hbm, intersections_ref),
                (owner_hbm, owner_ref),
                (weights_hbm, weights_ref),
            )
        )
    ]
    for load in loads:
        load.start()
    for load in loads[:5]:
        load.wait()
    count_entries(intersections_ref, owner_ref, counts_ref)
    mix_levels(fields_ref, bracket_ref, fraction_ref, mixed_ref)
    loads[5].wait()


def remap_kernel(mixed_ref, weights_ref, counts_ref, group_ref, cross_ref, far_ref, parts_ref):
    lev_dev, rows, blocks, cols = mixed_ref.shape
    cells = weights_ref.shape[2]
    interp = mixed_ref[0]
    for k in range(1, lev_dev):
        interp = interp + mixed_ref[k]
    interp = interp.reshape(rows * blocks, cols).astype(jnp.bfloat16)
    for w in range(weights_ref.shape[0]):
        part = jnp.dot(interp, weights_ref[w], preferred_element_type=jnp.float32)
        for r in range(rows):
            parts_ref[w * blocks : (w + 1) * blocks, r * cells : (r + 1) * cells] = part[
                r * blocks : (r + 1) * blocks
            ]
    counts = counts_ref[...].astype(jnp.bfloat16)
    parts = parts_ref[...]
    high = parts.astype(jnp.bfloat16)
    rest = parts - high.astype(jnp.float32)
    middle = rest.astype(jnp.bfloat16)
    low = (rest - middle.astype(jnp.float32)).astype(jnp.bfloat16)
    total = (
        jnp.dot(counts, low, preferred_element_type=jnp.float32)
        + jnp.dot(counts, middle, preferred_element_type=jnp.float32)
        + jnp.dot(counts, high, preferred_element_type=jnp.float32)
    )
    n_group = group_ref.shape[0]
    n_cross = cross_ref.shape[0]
    group_ref[...] = total[:n_group]
    cross_ref[...] = total[n_group : n_group + n_cross]
    far_ref[...] = total[n_group + n_cross :]


def join_kernel(group_ref, cross_ref, out_ref):
    tile_dev = cross_ref.shape[0] // CROSS
    upper = lax.axis_index("col") % GROUP >= CROSS
    for i in range(GROUP):
        member = (i + NEAR_FIRST) % GROUP
        mine = upper if member >= CROSS else jnp.logical_not(upper)
        start = member % CROSS * tile_dev
        forwarded = cross_ref[start : start + tile_dev]
        rows = slice(i * tile_dev, (i + 1) * tile_dev)
        out_ref[rows] = group_ref[rows] + jnp.where(mine, forwarded, 0.0)


def filter_kernel(near_ref, far_ref, late_ref, filtered_ref, stats_ref):
    tile_dev = far_ref.shape[0]
    rows = filtered_ref.shape[0]
    cells = filtered_ref.shape[2]
    total = far_ref[...] + late_ref[...]
    for k in range(near_ref.shape[0] // tile_dev):
        total = total + near_ref[k * tile_dev : (k + 1) * tile_dev]
    lane = lax.broadcasted_iota(jnp.int32, (1, cells), 1)
    stats = jnp.zeros((1, cells), jnp.float32)
    for r in range(rows):
        x = total[:, r * cells : (r + 1) * cells]
        left = jnp.concatenate([x[:, :1], x[:, :-1]], axis=1)
        right = jnp.concatenate([x[:, 1:], x[:, -1:]], axis=1)
        y = 0.25 * left + 0.5 * x + 0.25 * right
        filtered_ref[r] = y
        mean = jnp.sum(jnp.sum(y, axis=0, keepdims=True), axis=1, keepdims=True) / float(tile_dev * cells)
        off = y - mean
        spread = jnp.sum(jnp.sum(off * off, axis=0, keepdims=True), axis=1, keepdims=True)
        stats = jnp.where(lane == r, mean, jnp.where(lane == rows + r, spread, stats))
    stats_ref[...] = jnp.broadcast_to(stats, stats_ref.shape)


def normalize_kernel(stats_ref, filtered_ref, out_ref):
    rows, tile_dev, cells = filtered_ref.shape
    devices = stats_ref.shape[0]
    count = float(tile_dev * cells)
    stats = stats_ref[...]
    mean = jnp.sum(stats, axis=0, keepdims=True) / float(devices)
    apart = stats - mean
    between = jnp.sum(apart * apart, axis=0, keepdims=True)
    within = mean * float(devices)
    for r in range(rows):
        spread = within[:, rows + r : rows + r + 1] + count * between[:, r : r + 1]
        scale = lax.rsqrt(spread / (count * float(devices)) + epsilon)
        out_ref[r] = (filtered_ref[r] - mean[:, r : r + 1]) * scale


def remap_step(fields, bracket, fraction, remap_weights, intersections, tile_owner):
    lev_dev = lax.axis_size("lev")
    col_count = lax.axis_size("col")
    plev_dev = PLEV // lev_dev
    weights_dev, block_cols, tile_cells = remap_weights.shape
    blocks = fields.shape[2] // block_cols
    tile_dev = tile_owner.shape[0] // col_count
    rows = F * plev_dev
    f32 = jnp.float32

    n_group = GROUP * tile_dev
    n_cross = CROSS * tile_dev
    owner = tile_owner.reshape(-1, 128)
    sources = (fields, bracket, fraction, intersections, owner, remap_weights)
    anywhere = pl.BlockSpec(memory_space=pltpu.HBM)
    mixed, counts, weights = pl.pallas_call(
        prepare_kernel,
        in_specs=[anywhere] * 6,
        out_shape=[
            jax.ShapeDtypeStruct((lev_dev, rows, blocks, block_cols), f32),
            jax.ShapeDtypeStruct((n_group + n_cross + tile_dev, weights_dev * blocks), f32),
            jax.ShapeDtypeStruct(remap_weights.shape, remap_weights.dtype),
        ],
        scratch_shapes=[
            pltpu.VMEM(fields.shape, fields.dtype),
            pltpu.VMEM(bracket.shape, bracket.dtype),
            pltpu.VMEM(fraction.shape, fraction.dtype),
            pltpu.VMEM(intersections.shape, intersections.dtype),
            pltpu.VMEM(owner.shape, owner.dtype),
            pltpu.SemaphoreType.DMA((6,)),
        ],
        name="mix_and_count",
        compiler_params=PARAMS,
    )(*[pltpu.with_memory_space_constraint(x, pltpu.HBM) for x in sources])
    levs = [[(k + LEV_FIRST) % lev_dev for k in range(lev_dev)]]
    mixed = lax.all_to_all(mixed, "lev", 0, 0, tiled=True, axis_index_groups=levs)

    group, cross, far = pl.pallas_call(
        remap_kernel,
        out_shape=[
            jax.ShapeDtypeStruct((n, rows * tile_cells), f32) for n in (n_group, n_cross, tile_dev)
        ],
        scratch_shapes=[pltpu.VMEM((weights_dev * blocks, rows * tile_cells), f32)],
        name="remap_blocks",
        compiler_params=PARAMS,
    )(mixed, weights, counts)

    swap = [
        (d, (d - CROSS) % col_count if d % GROUP < CROSS else (d + CROSS) % col_count)
        for d in range(col_count)
    ]
    opposite = [(d, (d + col_count // 2) % col_count) for d in range(col_count)]
    early = [pair for pair in opposite if pair[0] % ROW < EARLY]
    late = [pair for pair in opposite if pair[0] % ROW >= EARLY]
    groups = [[g * GROUP + (k + NEAR_FIRST) % GROUP for k in range(GROUP)] for g in range(col_count // GROUP)]
    far_a = lax.ppermute(far, "col", early)
    far_b = lax.ppermute(far, "col", late)
    cross = lax.ppermute(cross, "col", swap)
    near = pl.pallas_call(
        join_kernel,
        out_shape=jax.ShapeDtypeStruct((n_group, rows * tile_cells), f32),
        name="join_forwarded",
        compiler_params=PARAMS,
    )(group, cross)
    near = lax.all_to_all(near, "col", 0, 0, tiled=True, axis_index_groups=groups)

    filtered, stats = pl.pallas_call(
        filter_kernel,
        out_shape=[
            jax.ShapeDtypeStruct((rows, tile_dev, tile_cells), f32),
            jax.ShapeDtypeStruct((col_count, tile_cells), f32),
        ],
        name="filter_tiles",
        compiler_params=PARAMS,
    )(near, far_a, far_b)
    lead = STATS_FIRST
    order = sorted(range(col_count), key=lambda d: (d != lead, d % ROW, d))
    stats = stats.reshape(col_count, 1, tile_cells)
    stats = lax.all_to_all(stats, "col", 0, 0, tiled=True, axis_index_groups=[order])
    normalized = pl.pallas_call(
        normalize_kernel,
        out_shape=jax.ShapeDtypeStruct(filtered.shape, f32),
        name="normalize_tiles",
        compiler_params=PARAMS,
    )(stats.reshape(col_count, tile_cells), filtered)
    return normalized.reshape(F, plev_dev, tile_dev, tile_cells)


def solution(mesh):
    in_specs = (
        P(None, "lev", "col"),
        P(None, "col"),
        P(None, "col"),
        P("col", None, None),
        P(None, "col"),
        P(),
    )
    out_specs = P(None, "lev", "col", None)
    return jax.shard_map(
        remap_step, mesh=mesh, in_specs=in_specs, out_specs=out_specs, check_vma=False
    )
```
